32 devices in a mesh: dp: 4 (over y, x), loop: 8 (over z, core).
Axes of the slice: x: 2, y: 2, z: 4, core: 2. Of those that a mesh axis runs over, the one named last changes fastest.
Arguments:
- features: bfloat16 [24, 7, 7, 2048], P('loop'), may hold values from -6 to 6
- image_ids: int32 [24], P('loop'), may hold values from 0 to 15
- text_embeds: bfloat16 [16, 1152], P('loop'), may hold values from -6 to 6
- text_ids: int32 [16], replicated, may hold values from 0 to 15, each once
- depth_kernel: bfloat16 [7, 7, 2048], replicated, may hold values from -0.875 to 0.875
- depth_bias: float32 [2048], replicated, may hold values from -3 to 3
- norm_gain: float32 [2048], replicated, may hold values from 0.5 to 2
- w_up: bfloat16 [2048, 4096], P(None, 'dp'), may hold values from -0.125 to 0.125
- w_down: bfloat16 [2048, 4096], P(None, 'dp'), may hold values from -0.09375 to 0.09375
- projection: bfloat16 [2048, 1152], replicated, may hold values from -0.125 to 0.125
- logit_scale: float32 [1], replicated, may hold values from 4 to 16
- logit_bias: float32 [1], replicated, may hold values from -4 to -1
Outputs:
- row_loss: float32 [24], P('loop')
- grad_texts: float32 [16, 1152], P('loop')
- grad_kernel: float32 [7, 7, 2048], replicated
- grad_bias: float32 [2048], replicated
- grad_gain: float32 [2048], replicated
- grad_up: float32 [2048, 4096], P('loop', 'dp')
- grad_down: float32 [2048, 4096], P('loop', 'dp')
- grad_proj: float32 [2048, 1152], P(('dp', 'loop'))
The draws below stay inside these ranges and needn't reach their ends.
Inputs may be any that keep to these rules, and one draw needn't show every extreme that they name: `image_ids`: each image's pair id names one text. `text_ids`: the 16 texts carry distinct pair ids.
All inputs are finite; a program needn't handle non-finite values.
Results may differ from the reference program's by a relative error of at most 0.0065.
Values sent between devices are 32-bit elements; how exact they have to be, the bound alone decides.
A program may use at most 192 MiB of HBM per device.

```python
import math
import jax
import jax.numpy as jnp
from jax import lax

C = 2048
HID = 4096
E = 1152
KERNEL = 7
GRID = 7
IMG_DEV = 3
IMAGES = 24
TEXTS = 16
N_LOOP = 8


def with_ends(array, own_key, low, top_value):
    extent = array.shape
    spot = [jax.random.randint(jax.random.fold_in(own_key, axis), (), 0, extent[axis]) for axis in range(len(extent))]
    array = array.at[tuple(spot)].set(low)
    longest = extent.index(max(extent))
    spot[longest] = (spot[longest] + 1) % extent[longest]
    return array.at[tuple(spot)].set(top_value)


def block_scale(rng, extent, pieces, low, high):
    loudness = 1.0
    for axis_at, parts in pieces:
        heights = jax.random.uniform(jax.random.fold_in(jax.random.fold_in(rng, 6), axis_at), (parts,), jnp.float32, low / len(pieces), high / len(pieces))
        loudness = loudness * jnp.repeat(jnp.exp(heights), extent[axis_at] // parts).reshape((-1,) + (1,) * (len(extent) - 1 - axis_at))
    return loudness


def gaussian(own_key, shape, scale, bound, shards=(), dtype=jnp.bfloat16):
    drawn = jax.random.normal(own_key, shape, jnp.float32) * scale
    if len(shards) > 0:
        drawn = block_scale(own_key, shape, shards, -0.22, 0.18) * drawn
    return jnp.clip(drawn, min=-bound, max=bound).astype(dtype)


def setup_inputs(seed: int = 0) -> dict:
    key_list = jax.random.split(jax.random.key(seed), 13)
    features = gaussian(key_list[0], (IMAGES, GRID, GRID, C), 1.0, 6.0, ((0, 8),))
    image_ids = with_ends(jax.random.randint(key_list[1], (IMAGES,), 0, TEXTS), jax.random.fold_in(key_list[1], 1), 0, TEXTS - 1).astype(jnp.int32)
    text_embeds = gaussian(key_list[2], (TEXTS, E), 1.0, 6.0, ((0, 8),))
    text_ids = jax.random.permutation(key_list[3], TEXTS).astype(jnp.int32)
    depth_kernel = gaussian(key_list[4], (KERNEL, KERNEL, C), (KERNEL * KERNEL) ** -0.5, 0.875)
    depth_bias = gaussian(key_list[5], (C,), 0.5, 3.0, (), jnp.float32)
    norm_gain = jnp.clip(jnp.exp(jax.random.uniform(key_list[6], (C,), jnp.float32, math.log(0.5), math.log(2.0))), 0.5, 2.0)
    w_up = gaussian(key_list[7], (C, HID), C ** -0.5, 0.125, ((1, 4),))
    w_down = gaussian(key_list[8], (C, HID), HID ** -0.5, 0.09375, ((1, 4),))
    projection = gaussian(key_list[9], (C, E), C ** -0.5, 0.125)
    logit_scale = jnp.clip(jnp.exp(jax.random.uniform(key_list[10], (1,), jnp.float32, math.log(4.0), math.log(16.0))), 4.0, 16.0)
    logit_bias = jnp.clip(jax.random.uniform(key_list[11], (1,), jnp.float32, -4.0, -1.0), -4.0, -1.0)
    return dict(features=features, image_ids=image_ids, text_embeds=text_embeds, text_ids=text_ids, depth_kernel=depth_kernel, depth_bias=depth_bias, norm_gain=norm_gain, w_up=w_up, w_down=w_down, projection=projection, logit_scale=logit_scale, logit_bias=logit_bias)


full_precision = lax.Precision.HIGHEST
half_root = 0.7071067811865476
density_factor = 0.3989422804014327

def gelu_value(values):
    return 0.5 * values * (1.0 + lax.erf(values * half_root))

def gelu_slope(values):
    cumulative = 0.5 * (1.0 + lax.erf(values * half_root))
    return cumulative + values * jnp.exp(-0.5 * values * values) * density_factor

def depthwise(images, kernel):
    side = kernel.shape[0]
    reach = (side - 1) // 2
    height = images.shape[1]
    width = images.shape[2]
    padded = jnp.pad(images, ((0, 0), (reach, reach), (reach, reach), (0, 0)))
    total = jnp.zeros(images.shape, jnp.float32)
    for row_off in range(side):
        for col_off in range(side):
            total = total + padded[:, row_off:row_off + height, col_off:col_off + width, :] * kernel[row_off, col_off]
    return total

def kernel_grad(images, grad_conv, side):
    reach = (side - 1) // 2
    height = images.shape[1]
    width = images.shape[2]
    padded = jnp.pad(images, ((0, 0), (reach, reach), (reach, reach), (0, 0)))
    rows_out = []
    for row_off in range(side):
        cols_out = []
        for col_off in range(side):
            window = padded[:, row_off:row_off + height, col_off:col_off + width, :]
            cols_out.append(lax.optimization_barrier(jnp.sum(window * grad_conv, axis=(0, 1, 2))))
        rows_out.append(jnp.stack(cols_out, axis=0))
    return jnp.stack(rows_out, axis=0)

def norm_parts(images, depth_kernel, depth_bias, norm_gain):
    conv_out = depthwise(images.astype(jnp.float32), depth_kernel.astype(jnp.float32)) + depth_bias
    centered = conv_out - lax.optimization_barrier(jnp.mean(conv_out, axis=3, keepdims=True))
    inv_std = lax.rsqrt(lax.optimization_barrier(jnp.mean(centered * centered, axis=3, keepdims=True)) + 1e-06)
    unit_part = centered * inv_std
    normed = (unit_part * norm_gain).astype(jnp.bfloat16)
    return (unit_part, inv_std, normed)

def unit_rows(values):
    inverse = lax.rsqrt(lax.optimization_barrier(jnp.sum(values * values, axis=1, keepdims=True)) + 1e-06)
    return (values * inverse, inverse)

def conv_grads(images, depth_kernel, unit_part, inv_std, norm_gain, grad_normed):
    grad_gain = lax.optimization_barrier(jnp.sum(grad_normed * unit_part, axis=(0, 1, 2)))
    grad_unit = grad_normed * norm_gain
    grad_conv = inv_std * (grad_unit - lax.optimization_barrier(jnp.mean(grad_unit, axis=3, keepdims=True)) - unit_part * lax.optimization_barrier(jnp.mean(grad_unit * unit_part, axis=3, keepdims=True)))
    grad_bias = lax.optimization_barrier(jnp.sum(grad_conv, axis=(0, 1, 2)))
    grad_kernel = kernel_grad(images.astype(jnp.float32), grad_conv, depth_kernel.shape[0])
    return (grad_kernel, grad_bias, grad_gain)

def reference(features, image_ids, text_embeds, text_ids, depth_kernel, depth_bias, norm_gain, w_up, w_down, projection, logit_scale, logit_bias):
    cell_count = GRID * GRID
    groups = features.reshape(N_LOOP, IMG_DEV, GRID, GRID, C)

    def forward_one(images):
        unit_part, inv_std, normed = norm_parts(images, depth_kernel, depth_bias, norm_gain)
        pre_act = jnp.dot(normed.reshape(-1, C), w_up, preferred_element_type=jnp.float32)
        hidden_mean = lax.optimization_barrier(jnp.mean(gelu_value(pre_act).reshape(IMG_DEV, cell_count, HID), axis=1)).astype(jnp.bfloat16)
        mlp_pool = lax.dot_general(hidden_mean, w_down, (((1,), (1,)), ((), ())), preferred_element_type=jnp.float32)
        pooled = (lax.optimization_barrier(jnp.mean(images.astype(jnp.float32), axis=(1, 2))) + mlp_pool).astype(jnp.bfloat16)
        return (pooled, hidden_mean)
    pooled, hidden_mean = lax.map(forward_one, groups)
    pooled = pooled.reshape(IMAGES, C)
    hidden_mean = hidden_mean.reshape(IMAGES, HID)
    embedding = jnp.dot(pooled, projection, preferred_element_type=jnp.float32)
    scale_value = logit_scale[0]
    bias_value = logit_bias[0]
    image_unit, image_inverse = unit_rows(embedding)
    text_unit, text_inverse = unit_rows(text_embeds.astype(jnp.float32))
    logits = scale_value * jnp.dot(image_unit, text_unit.T, precision=full_precision) + bias_value
    labels = jnp.where(image_ids[:, None] == text_ids[None, :], 1.0, -1.0).astype(jnp.float32)
    row_loss = -lax.optimization_barrier(jnp.sum(jax.nn.log_sigmoid(labels * logits), axis=1))
    coeffs = -scale_value * labels * jax.nn.sigmoid(-labels * logits)
    grad_image = jnp.dot(coeffs, text_unit, precision=full_precision)
    grad_text = jnp.dot(coeffs.T, image_unit, precision=full_precision)
    grad_texts = text_inverse * (grad_text - text_unit * lax.optimization_barrier(jnp.sum(text_unit * grad_text, axis=1, keepdims=True)))
    grad_embed = (image_inverse * (grad_image - image_unit * lax.optimization_barrier(jnp.sum(image_unit * grad_image, axis=1, keepdims=True)))).astype(jnp.bfloat16)
    grad_pooled = lax.dot_general(grad_embed, projection, (((1,), (1,)), ((), ())), preferred_element_type=jnp.float32).astype(jnp.bfloat16)
    grad_proj = lax.dot_general(pooled, grad_embed, (((0,), (0,)), ((), ())), preferred_element_type=jnp.float32)
    grad_down = lax.dot_general(grad_pooled, hidden_mean, (((0,), (0,)), ((), ())), preferred_element_type=jnp.float32)
    grad_groups = grad_pooled.reshape(N_LOOP, IMG_DEV, C)

    def backward_step(carry_state, inputs_pair):
        up_total, kernel_total, bias_total, gain_total = carry_state
        images, group_grad = inputs_pair
        unit_part, inv_std, normed = norm_parts(images, depth_kernel, depth_bias, norm_gain)
        normed_rows = normed.reshape(-1, C)
        pre_act = jnp.dot(normed_rows, w_up, preferred_element_type=jnp.float32)
        spread = jnp.dot(group_grad, w_down, preferred_element_type=jnp.float32) / cell_count
        grad_pre = (gelu_slope(pre_act).reshape(IMG_DEV, cell_count, HID) * spread[:, None, :]).reshape(-1, HID).astype(jnp.bfloat16)
        up_part = lax.dot_general(normed_rows, grad_pre, (((0,), (0,)), ((), ())), preferred_element_type=jnp.float32)
        grad_normed = lax.dot_general(grad_pre, w_up, (((1,), (1,)), ((), ())), preferred_element_type=jnp.float32).reshape(images.shape)
        kernel_part, bias_part, gain_part = conv_grads(images, depth_kernel, unit_part, inv_std, norm_gain, grad_normed)
        return ((up_total + up_part, kernel_total + kernel_part, bias_total + bias_part, gain_total + gain_part), jnp.zeros((), jnp.float32))
    start_state = (jnp.zeros((C, HID), jnp.float32), jnp.zeros((KERNEL, KERNEL, C), jnp.float32), jnp.zeros((C,), jnp.float32), jnp.zeros((C,), jnp.float32))
    totals, unused = lax.scan(backward_step, start_state, (groups, grad_groups))
    return (row_loss, grad_texts, totals[1], totals[2], totals[3], totals[0], grad_down, grad_proj)
```

```python
import functools
import jax
import jax.numpy as jnp
from jax import lax
from jax.experimental import pallas as pl
from jax.experimental.pallas import tpu as pltpu
from jax.sharding import PartitionSpec as P

GRID = 7
LANES = 128
ROWS = 8

full_precision = lax.Precision.HIGHEST
half_root = 0.7071067811865476
density_factor = 0.3989422804014327


def gelu_value(values):
    return 0.5 * values * (1.0 + lax.erf(values * half_root))


def gelu_slope(values):
    cumulative = 0.5 * (1.0 + lax.erf(values * half_root))
    return cumulative + values * jnp.exp(-0.5 * values * values) * density_factor


def unit_rows(values):
    inverse = lax.rsqrt(jnp.sum(values * values, axis=1, keepdims=True) + 1e-06)
    return (values * inverse, inverse)


def lane_tile(index):
    return pl.ds(pl.multiple_of(index * LANES, LANES), LANES)


def shifted_rows(x_ref, lanes, by, cell):
    count = x_ref.shape[0]
    moved = []
    for row in range(GRID):
        per_image = []
        for n in range(count):
            tile = x_ref[n, row, :, lanes]
            if by != 0:
                tile = pltpu.roll(tile, (-by) % ROWS, 0)
            if abs(by) > 1:
                inside = (cell + by >= 0) & (cell + by < GRID)
                tile = jnp.where(inside, tile, 0.0)
            per_image.append(tile)
        moved.append(per_image)
    return moved


def conv_norm_kernel(x_ref, k_ref, bias_ref, unit_ref, inv_ref):
    count = x_ref.shape[0]
    channels = x_ref.shape[3]
    tiles = channels // LANES
    reach = (GRID - 1) // 2
    cell = lax.broadcasted_iota(jnp.int32, (ROWS, LANES), 0)
    cells = [(n, p) for p in range(GRID) for n in range(count)]

    def conv_tile(index, sums):
        lanes = lane_tile(index)
        bias = jnp.broadcast_to(bias_ref[:, lanes], (ROWS, LANES))
        out = {at: bias for at in cells}
        for col_off in range(GRID):
            moved = shifted_rows(x_ref, lanes, col_off - reach, cell)
            for row_off in range(GRID):
                tap = row_off * GRID + col_off
                weight = jnp.broadcast_to(k_ref[tap : tap + 1, lanes], (ROWS, LANES))
                for p in range(GRID):
                    row = p + row_off - reach
                    if 0 <= row < GRID:
                        for n in range(count):
                            out[(n, p)] = out[(n, p)] + moved[row][n] * weight
        for n, p in cells:
            unit_ref[n, p, :, lanes] = out[(n, p)]
        return tuple(total + out[at] for total, at in zip(sums, cells))

    zeros = tuple(jnp.zeros((ROWS, LANES), jnp.float32) for _ in cells)
    sums = lax.fori_loop(0, tiles, conv_tile, zeros)
    means = [jnp.sum(total, axis=1, keepdims=True) / channels for total in sums]
    means = [jnp.broadcast_to(mean, (ROWS, LANES)) for mean in means]

    def square_tile(index, sums):
        lanes = lane_tile(index)
        result = []
        for total, mean, (n, p) in zip(sums, means, cells):
            centered = unit_ref[n, p, :, lanes] - mean
            result.append(total + centered * centered)
        return tuple(result)

    squares = lax.fori_loop(0, tiles, square_tile, zeros)
    inverses = []
    for total, (n, p) in zip(squares, cells):
        variance = jnp.sum(total, axis=1, keepdims=True) / channels
        inverse = jnp.broadcast_to(lax.rsqrt(variance + 1e-06), (ROWS, LANES))
        inverse = jnp.where(cell < GRID, inverse, 0.0)
        inv_ref[n, p, :, :] = inverse
        inverses.append(inverse)

    def norm_tile(index, carry):
        lanes = lane_tile(index)
        for inverse, mean, (n, p) in zip(inverses, means, cells):
            unit = (unit_ref[n, p, :, lanes] - mean) * inverse
            unit_ref[n, p, :, lanes] = unit
        return carry

    lax.fori_loop(0, tiles, norm_tile, 0)


def conv_norm(padded, taps, bias):
    count, _, _, channels = padded.shape
    whole = pl.BlockSpec(memory_space=pltpu.VMEM)
    full = jax.ShapeDtypeStruct(padded.shape, jnp.float32)
    return pl.pallas_call(
        conv_norm_kernel,
        out_shape=(
            full,
            jax.ShapeDtypeStruct((count, GRID, ROWS, LANES), jnp.float32),
        ),
        in_specs=[whole] * 3,
        out_specs=(whole, whole),
        compiler_params=pltpu.CompilerParams(vmem_limit_bytes=24 * 1024 * 1024),
        cost_estimate=pl.CostEstimate(
            flops=2 * 49 * padded.size, bytes_accessed=12 * padded.size, transcendentals=0
        ),
    )(padded, taps, bias)


def conv_grad_kernel(x_ref, unit_ref, inv_ref, gain_ref, grad_ref, out_ref, work_ref):
    count = x_ref.shape[0]
    channels = x_ref.shape[3]
    tiles = channels // LANES
    reach = (GRID - 1) // 2
    taps = GRID * GRID
    cell = lax.broadcasted_iota(jnp.int32, (ROWS, LANES), 0)
    cells = [(n, p) for p in range(GRID) for n in range(count)]
    zero = jnp.zeros((ROWS, LANES), jnp.float32)

    def first_tile(index, carry):
        plain, crossed = carry
        lanes = lane_tile(index)
        gain = jnp.broadcast_to(gain_ref[:, lanes], (ROWS, LANES))
        gain_sum = zero
        plain_out = []
        crossed_out = []
        for at, (n, p) in enumerate(cells):
            unit = unit_ref[n, p, :, lanes]
            grad = grad_ref[n, p, :, lanes]
            gain_sum = gain_sum + grad * unit
            scaled = grad * gain
            plain_out.append(plain[at] + scaled)
            crossed_out.append(crossed[at] + scaled * unit)
        out_ref[taps + 1 : taps + 2, lanes] = jnp.sum(gain_sum, axis=0, keepdims=True)
        return (tuple(plain_out), tuple(crossed_out))

    zeros = tuple(zero for _ in cells)
    plain, crossed = lax.fori_loop(0, tiles, first_tile, (zeros, zeros))
    for at, (n, p) in enumerate(cells):
        first = jnp.sum(plain[at], axis=1, keepdims=True) / channels
        second = jnp.sum(crossed[at], axis=1, keepdims=True) / channels
        work_ref[0, n, p, :, :] = jnp.broadcast_to(first, (ROWS, LANES))
        work_ref[1, n, p, :, :] = jnp.broadcast_to(second, (ROWS, LANES))

    def tap_tile(index, carry):
        lanes = lane_tile(index)
        gain = jnp.broadcast_to(gain_ref[:, lanes], (ROWS, LANES))
        grad_conv = {}
        bias_sum = zero
        for n, p in cells:
            value = inv_ref[n, p, :, :] * (
                grad_ref[n, p, :, lanes] * gain
                - work_ref[0, n, p, :, :]
                - unit_ref[n, p, :, lanes] * work_ref[1, n, p, :, :]
            )
            grad_conv[(n, p)] = value
            bias_sum = bias_sum + value
        out_ref[taps : taps + 1, lanes] = jnp.sum(bias_sum, axis=0, keepdims=True)
        for col_off in range(GRID):
            moved = shifted_rows(x_ref, lanes, col_off - reach, cell)
            for row_off in range(GRID):
                tap = row_off * GRID + col_off
                total = zero
                for p in range(GRID):
                    row = p + row_off - reach
                    if 0 <= row < GRID:
                        for n in range(count):
                            total = total + moved[row][n] * grad_conv[(n, p)]
                out_ref[tap : tap + 1, lanes] = jnp.sum(total, axis=0, keepdims=True)
        return carry

    lax.fori_loop(0, tiles, tap_tile, 0)


def conv_grads(padded, unit, inverse, gain, grad):
    count, _, _, channels = padded.shape
    whole = pl.BlockSpec(memory_space=pltpu.VMEM)
    return pl.pallas_call(
        conv_grad_kernel,
        out_shape=jax.ShapeDtypeStruct((GRID * GRID + 2, channels), jnp.float32),
        in_specs=[whole] * 5,
        out_specs=whole,
        scratch_shapes=[pltpu.VMEM((2, count, GRID, ROWS, LANES), jnp.float32)],
        compiler_params=pltpu.CompilerParams(vmem_limit_bytes=24 * 1024 * 1024),
        cost_estimate=pl.CostEstimate(
            flops=2 * 49 * padded.size, bytes_accessed=12 * padded.size, transcendentals=0
        ),
    )(padded, unit, inverse, gain, grad)


def on_device(
    features,
    image_ids,
    text_embeds,
    text_ids,
    depth_kernel,
    depth_bias,
    norm_gain,
    w_up,
    w_down,
    projection,
    logit_scale,
    logit_bias,
):
    image_rows = features.shape[0]
    channels = features.shape[3]
    hidden_share = w_up.shape[1]
    cell_count = GRID * GRID
    loop_count = lax.axis_size("loop")
    position = lax.axis_index("loop")
    image_count = image_rows * loop_count
    text_rows = text_embeds.shape[0]
    first_image = position * image_rows
    gather = functools.partial(lax.all_gather, axis_name="loop", axis=0, tiled=True)

    text_unit, text_inverse = unit_rows(text_embeds.astype(jnp.float32))
    cell_mean = jnp.mean(features.astype(jnp.float32), axis=(1, 2))
    text_all = gather(text_unit)
    mean_all = gather(cell_mean)
    ids_all = lax.all_gather(image_ids, "loop", axis=0, tiled=True)

    padded = jnp.pad(
        features.astype(jnp.float32), ((0, 0), (0, 0), (0, ROWS - GRID), (0, 0))
    )
    gain_row = norm_gain[None, :]
    unit, inverse = conv_norm(
        padded,
        depth_kernel.astype(jnp.float32).reshape(cell_count, channels),
        depth_bias[None, :],
    )
    padded_rows = image_rows * GRID * ROWS
    unit_rows_own = unit.reshape(padded_rows, channels)
    unit_share = lax.all_to_all(unit_rows_own, "loop", split_axis=1, concat_axis=0, tiled=True)
    normed_rows = (unit_rows_own * gain_row).astype(jnp.bfloat16)
    pre_act = jnp.dot(normed_rows, w_up, preferred_element_type=jnp.float32)
    hidden_sum = jnp.sum(
        gelu_value(pre_act).reshape(image_rows, GRID * ROWS, hidden_share), axis=1
    )
    slope = gelu_slope(pre_act)
    slope_all = gather(slope)
    hidden_all = (gather(hidden_sum) / cell_count).astype(jnp.bfloat16)
    mlp_part = lax.dot_general(
        hidden_all, w_down, (((1,), (1,)), ((), ())), preferred_element_type=jnp.float32
    )
    mlp_pool = lax.psum(mlp_part, "dp")
    pooled = (mean_all + mlp_pool).astype(jnp.bfloat16)
    embedding = jnp.dot(pooled, projection, preferred_element_type=jnp.float32)
    image_unit, image_inverse = unit_rows(embedding)
    logits = (
        logit_scale[0] * jnp.dot(image_unit, text_all.T, precision=full_precision)
        + logit_bias[0]
    )
    labels = jnp.where(ids_all[:, None] == text_ids[None, :], 1.0, -1.0).astype(jnp.float32)
    loss_all = -jnp.sum(jax.nn.log_sigmoid(labels * logits), axis=1)
    row_loss = lax.dynamic_slice_in_dim(loss_all, first_image, image_rows)
    coeffs = -logit_scale[0] * labels * jax.nn.sigmoid(-labels * logits)
    grad_image = jnp.dot(coeffs, text_all, precision=full_precision)
    own_coeffs = lax.dynamic_slice_in_dim(coeffs, position * text_rows, text_rows, 1)
    grad_text = jnp.dot(own_coeffs.T, image_unit, precision=full_precision)
    grad_texts = text_inverse * (
        grad_text - text_unit * jnp.sum(text_unit * grad_text, axis=1, keepdims=True)
    )
    grad_embed = (
        image_inverse
        * (grad_image - image_unit * jnp.sum(image_unit * grad_image, axis=1, keepdims=True))
    ).astype(jnp.bfloat16)
    grad_pooled = lax.dot_general(
        grad_embed, projection, (((1,), (1,)), ((), ())), preferred_element_type=jnp.float32
    ).astype(jnp.bfloat16)
    spread = jnp.dot(grad_pooled, w_down, preferred_element_type=jnp.float32) / cell_count
    own_spread = lax.dynamic_slice_in_dim(spread, first_image, image_rows)
    grad_pre = (
        (slope.reshape(image_rows, GRID * ROWS, hidden_share) * own_spread[:, None, :])
        .reshape(padded_rows, hidden_share)
        .astype(jnp.bfloat16)
    )
    grad_normed = lax.dot_general(
        grad_pre, w_up, (((1,), (1,)), ((), ())), preferred_element_type=jnp.float32
    ).reshape(padded.shape)
    part = conv_grads(padded, unit, inverse, gain_row, grad_normed)
    total = lax.psum(part, ("dp", "loop"))
    grad_kernel = total[:cell_count].reshape(GRID, GRID, channels)
    grad_bias = total[cell_count]
    grad_gain = total[cell_count + 1]

    up_share = channels // loop_count
    grad_pooled_share = lax.dynamic_slice_in_dim(grad_pooled, position * up_share, up_share, 1)
    grad_down = lax.dot_general(
        grad_pooled_share, hidden_all, (((0,), (0,)), ((), ())), preferred_element_type=jnp.float32
    )
    proj_share = up_share // lax.axis_size("dp")
    proj_at = (lax.axis_index("dp") * loop_count + position) * proj_share
    pooled_share = lax.dynamic_slice_in_dim(pooled, proj_at, proj_share, 1)
    grad_proj = lax.dot_general(
        pooled_share, grad_embed, (((0,), (0,)), ((), ())), preferred_element_type=jnp.float32
    )
    grad_pre_all = (
        (slope_all.reshape(image_count, GRID * ROWS, hidden_share) * spread[:, None, :])
        .reshape(loop_count * padded_rows, hidden_share)
        .astype(jnp.bfloat16)
    )
    gain_share = lax.dynamic_slice_in_dim(norm_gain, position * up_share, up_share)
    normed_share = (unit_share * gain_share).astype(jnp.bfloat16)
    grad_up = lax.dot_general(
        normed_share,
        grad_pre_all,
        (((0,), (0,)), ((), ())),
        preferred_element_type=jnp.float32,
    )
    return (row_loss, grad_texts, grad_kernel, grad_bias, grad_gain, grad_up, grad_down, grad_proj)


def solution(mesh):
    placed = (
        P("loop", None, None, None),
        P("loop"),
        P("loop", None),
        P(),
        P(),
        P(),
        P(),
        P(None, "dp"),
        P(None, "dp"),
        P(),
        P(),
        P(),
    )
    return jax.shard_map(
        on_device,
        mesh=mesh,
        in_specs=placed,
        out_specs=(
            P("loop"),
            P("loop", None),
            P(),
            P(),
            P(),
            P("loop", "dp"),
            P("loop", "dp"),
            P(("dp", "loop"), None),
        ),
        check_vma=False,
    )
```

```python
import functools
import jax
import jax.numpy as jnp
from jax import lax
from jax.experimental import pallas as pl
from jax.experimental.pallas import tpu as pltpu
from jax.sharding import PartitionSpec as P

GRID = 7
LANES = 128
ROWS = 8
TAP_ROWS = 64

full_precision = lax.Precision.HIGHEST
half_root = 0.7071067811865476
density_factor = 0.3989422804014327


def gelu_value(values):
    return 0.5 * values * (1.0 + lax.erf(values * half_root))


def gelu_slope(values):
    cumulative = 0.5 * (1.0 + lax.erf(values * half_root))
    return cumulative + values * jnp.exp(-0.5 * values * values) * density_factor


def unit_rows(values):
    inverse = lax.rsqrt(jnp.sum(values * values, axis=1, keepdims=True) + 1e-06)
    return (values * inverse, inverse)


def lane_tile(index):
    return pl.ds(pl.multiple_of(index * LANES, LANES), LANES)


def shifted_rows(x_ref, lanes, by, cell):
    count = x_ref.shape[0]
    moved = []
    for row in range(GRID):
        per_image = []
        for n in range(count):
            tile = x_ref[n, row, :, lanes]
            if by != 0:
                tile = pltpu.roll(tile, (-by) % ROWS, 0)
            if abs(by) > 1:
                inside = (cell + by >= 0) & (cell + by < GRID)
                tile = jnp.where(inside, tile, 0.0)
            per_image.append(tile)
        moved.append(per_image)
    return moved


def conv_norm_kernel(x_ref, k_ref, bias_ref, unit_ref, inv_ref):
    count = x_ref.shape[0]
    channels = x_ref.shape[3]
    tiles = channels // LANES
    reach = (GRID - 1) // 2
    cell = lax.broadcasted_iota(jnp.int32, (ROWS, LANES), 0)
    cells = [(n, p) for p in range(GRID) for n in range(count)]

    def conv_tile(index, sums):
        lanes = lane_tile(index)
        bias = jnp.broadcast_to(bias_ref[:, lanes], (ROWS, LANES))
        out = {at: bias for at in cells}
        for col_off in range(GRID):
            moved = shifted_rows(x_ref, lanes, col_off - reach, cell)
            for row_off in range(GRID):
                tap = row_off * GRID + col_off
                weight = jnp.broadcast_to(k_ref[tap : tap + 1, lanes], (ROWS, LANES))
                for p in range(GRID):
                    row = p + row_off - reach
                    if 0 <= row < GRID:
                        for n in range(count):
                            out[(n, p)] = out[(n, p)] + moved[row][n] * weight
        for n, p in cells:
            unit_ref[n, p, :, lanes] = out[(n, p)]
        return tuple(total + out[at] for total, at in zip(sums, cells))

    zeros = tuple(jnp.zeros((ROWS, LANES), jnp.float32) for _ in cells)
    sums = lax.fori_loop(0, tiles, conv_tile, zeros)
    means = [jnp.sum(total, axis=1, keepdims=True) / channels for total in sums]
    means = [jnp.broadcast_to(mean, (ROWS, LANES)) for mean in means]

    def square_tile(index, sums):
        lanes = lane_tile(index)
        result = []
        for total, mean, (n, p) in zip(sums, means, cells):
            centered = unit_ref[n, p, :, lanes] - mean
            result.append(total + centered * centered)
        return tuple(result)

    squares = lax.fori_loop(0, tiles, square_tile, zeros)
    inverses = []
    for total, (n, p) in zip(squares, cells):
        variance = jnp.sum(total, axis=1, keepdims=True) / channels
        inverse = jnp.broadcast_to(lax.rsqrt(variance + 1e-06), (ROWS, LANES))
        inverse = jnp.where(cell < GRID, inverse, 0.0)
        inv_ref[n, p, :, :] = inverse
        inverses.append(inverse)

    def norm_tile(index, carry):
        lanes = lane_tile(index)
        for inverse, mean, (n, p) in zip(inverses, means, cells):
            unit = (unit_ref[n, p, :, lanes] - mean) * inverse
            unit_ref[n, p, :, lanes] = unit
        return carry

    lax.fori_loop(0, tiles, norm_tile, 0)


def conv_norm(padded, taps, bias):
    count, _, _, channels = padded.shape
    whole = pl.BlockSpec(memory_space=pltpu.VMEM)
    full = jax.ShapeDtypeStruct(padded.shape, jnp.float32)
    return pl.pallas_call(
        conv_norm_kernel,
        out_shape=(
            full,
            jax.ShapeDtypeStruct((count, GRID, ROWS, LANES), jnp.float32),
        ),
        in_specs=[whole] * 3,
        out_specs=(whole, whole),
        compiler_params=pltpu.CompilerParams(vmem_limit_bytes=24 * 1024 * 1024),
    )(padded, taps, bias)


def conv_grad_kernel(x_ref, unit_ref, inv_ref, gain_ref, grad_ref, out_ref, work_ref):
    count = x_ref.shape[0]
    channels = x_ref.shape[3]
    tiles = channels // LANES
    reach = (GRID - 1) // 2
    taps = GRID * GRID
    cell = lax.broadcasted_iota(jnp.int32, (ROWS, LANES), 0)
    cells = [(n, p) for p in range(GRID) for n in range(count)]
    zero = jnp.zeros((ROWS, LANES), jnp.float32)

    def first_tile(index, carry):
        plain, crossed = carry
        lanes = lane_tile(index)
        gain = jnp.broadcast_to(gain_ref[:, lanes], (ROWS, LANES))
        gain_sum = zero
        out_ref[index, 48:TAP_ROWS, :] = jnp.zeros((TAP_ROWS - 48, LANES), jnp.float32)
        plain_out = []
        crossed_out = []
        for at, (n, p) in enumerate(cells):
            unit = unit_ref[n, p, :, lanes]
            grad = grad_ref[n, p, :, lanes]
            gain_sum = gain_sum + grad * unit
            scaled = grad * gain
            plain_out.append(plain[at] + scaled)
            crossed_out.append(crossed[at] + scaled * unit)
        out_ref[index, taps + 1 : taps + 2, :] = jnp.sum(gain_sum, axis=0, keepdims=True)
        return (tuple(plain_out), tuple(crossed_out))

    zeros = tuple(zero for _ in cells)
    plain, crossed = lax.fori_loop(0, tiles, first_tile, (zeros, zeros))
    for at, (n, p) in enumerate(cells):
        first = jnp.sum(plain[at], axis=1, keepdims=True) / channels
        second = jnp.sum(crossed[at], axis=1, keepdims=True) / channels
        work_ref[0, n, p, :, :] = jnp.broadcast_to(first, (ROWS, LANES))
        work_ref[1, n, p, :, :] = jnp.broadcast_to(second, (ROWS, LANES))

    def tap_tile(index, carry):
        lanes = lane_tile(index)
        gain = jnp.broadcast_to(gain_ref[:, lanes], (ROWS, LANES))
        grad_conv = {}
        bias_sum = zero
        for n, p in cells:
            value = inv_ref[n, p, :, :] * (
                grad_ref[n, p, :, lanes] * gain
                - work_ref[0, n, p, :, :]
                - unit_ref[n, p, :, lanes] * work_ref[1, n, p, :, :]
            )
            grad_conv[(n, p)] = value
            bias_sum = bias_sum + value
        out_ref[index, taps : taps + 1, :] = jnp.sum(bias_sum, axis=0, keepdims=True)
        for col_off in range(GRID):
            moved = shifted_rows(x_ref, lanes, col_off - reach, cell)
            for row_off in range(GRID):
                tap = row_off * GRID + col_off
                total = zero
                for p in range(GRID):
                    row = p + row_off - reach
                    if 0 <= row < GRID:
                        for n in range(count):
                            total = total + moved[row][n] * grad_conv[(n, p)]
                out_ref[index, tap : tap + 1, :] = jnp.sum(total, axis=0, keepdims=True)
        return carry

    lax.fori_loop(0, tiles, tap_tile, 0)


def conv_grads(padded, unit, inverse, gain, grad):
    count, _, _, channels = padded.shape
    whole = pl.BlockSpec(memory_space=pltpu.VMEM)
    return pl.pallas_call(
        conv_grad_kernel,
        out_shape=jax.ShapeDtypeStruct((channels // LANES, TAP_ROWS, LANES), jnp.float32),
        in_specs=[whole] * 5,
        out_specs=whole,
        scratch_shapes=[pltpu.VMEM((2, count, GRID, ROWS, LANES), jnp.float32)],
        compiler_params=pltpu.CompilerParams(vmem_limit_bytes=24 * 1024 * 1024),
    )(padded, unit, inverse, gain, grad)


def peer_copies(axis, count, source_of, target, send_sems, recv_sems):
    me = lax.axis_index(axis)
    copies = []
    for by in range(1, count):
        peer = lax.rem(me + by, count)
        copy = pltpu.make_async_remote_copy(
            src_ref=source_of(peer),
            dst_ref=target.at[me],
            send_sem=send_sems.at[by],
            recv_sem=recv_sems.at[by],
            device_id={axis: peer},
            device_id_type=pl.DeviceIdType.MESH,
        )
        copy.start()
        copies.append(copy)
    return copies


def wait_all(copies):
    for copy in copies:
        copy.wait()


def meet_peers(sizes):
    barrier = pltpu.get_barrier_semaphore()
    total = 0
    for axis, count in sizes:
        me = lax.axis_index(axis)
        for by in range(1, count):
            pl.semaphore_signal(
                barrier,
                inc=1,
                device_id={axis: lax.rem(me + by, count)},
                device_id_type=pl.DeviceIdType.MESH,
            )
        total += count - 1
    pl.semaphore_wait(barrier, total)


def head_kernel(
    dp, loop, part_ref, mean_ref, rest_ref, pooled_ref, rest_out_ref, parts, own, sems
):
    meet_peers((("dp", dp), ("loop", loop)))
    loop_me = lax.axis_index("loop")
    dp_me = lax.axis_index("dp")
    dp_copies = peer_copies(
        "dp", dp, lambda peer: part_ref, parts, sems.at[0], sems.at[1]
    )
    rest_copies = peer_copies(
        "loop", loop, lambda peer: rest_ref, rest_out_ref, sems.at[2], sems.at[3]
    )
    parts[dp_me] = part_ref[...]
    rest_out_ref[loop_me] = rest_ref[...]
    wait_all(dp_copies)
    total = parts[0]
    for at in range(1, dp):
        total = total + parts[at]
    own[...] = mean_ref[...] + total
    pooled_copies = peer_copies(
        "loop", loop, lambda peer: own, pooled_ref, sems.at[4], sems.at[5]
    )
    pooled_ref[loop_me] = own[...]
    wait_all(rest_copies)
    wait_all(pooled_copies)


def head_exchange(part, mean, rest):
    dp = lax.axis_size("dp")
    loop = lax.axis_size("loop")
    whole = pl.BlockSpec(memory_space=pltpu.VMEM)
    return pl.pallas_call(
        functools.partial(head_kernel, dp, loop),
        out_shape=(
            jax.ShapeDtypeStruct((loop,) + part.shape, jnp.float32),
            jax.ShapeDtypeStruct((loop,) + rest.shape, jnp.float32),
        ),
        in_specs=[whole] * 3,
        out_specs=(whole, whole),
        scratch_shapes=[
            pltpu.VMEM((dp,) + part.shape, jnp.float32),
            pltpu.VMEM(part.shape, jnp.float32),
            pltpu.SemaphoreType.DMA((6, max(dp, loop))),
        ],
        compiler_params=pltpu.CompilerParams(
            collective_id=0, has_side_effects=True, vmem_limit_bytes=16 * 1024 * 1024
        ),
    )(part, mean, rest)


def total_kernel(dp, loop, part_ref, out_ref, dp_slots, loop_slots, block, chunk, sems):
    meet_peers((("dp", dp), ("loop", loop)))
    loop_me = lax.axis_index("loop")
    dp_me = lax.axis_index("dp")
    copies = peer_copies(
        "dp", dp, lambda peer: part_ref.at[peer], dp_slots, sems.at[0], sems.at[1]
    )
    dp_slots[dp_me] = part_ref[dp_me]
    wait_all(copies)
    total = dp_slots[0]
    for at in range(1, dp):
        total = total + dp_slots[at]
    block[...] = total
    copies = peer_copies(
        "loop", loop, lambda peer: block.at[peer], loop_slots, sems.at[2], sems.at[3]
    )
    loop_slots[loop_me] = block[loop_me]
    wait_all(copies)
    total = loop_slots[0]
    for at in range(1, loop):
        total = total + loop_slots[at]
    chunk[...] = total
    mine = out_ref.at[dp_me]
    copies = peer_copies("loop", loop, lambda peer: chunk, mine, sems.at[4], sems.at[5])
    out_ref[dp_me, loop_me] = chunk[...]
    wait_all(copies)
    copies = peer_copies("dp", dp, lambda peer: mine, out_ref, sems.at[6], sems.at[7])
    wait_all(copies)


def total_sum(part):
    dp = lax.axis_size("dp")
    loop = lax.axis_size("loop")
    rows = part.shape[0] * part.shape[1] // (dp * loop)
    whole = pl.BlockSpec(memory_space=pltpu.VMEM)
    summed = pl.pallas_call(
        functools.partial(total_kernel, dp, loop),
        out_shape=jax.ShapeDtypeStruct((dp, loop, rows, LANES), jnp.float32),
        in_specs=[whole],
        out_specs=whole,
        scratch_shapes=[
            pltpu.VMEM((dp, loop, rows, LANES), jnp.float32),
            pltpu.VMEM((loop, rows, LANES), jnp.float32),
            pltpu.VMEM((loop, rows, LANES), jnp.float32),
            pltpu.VMEM((rows, LANES), jnp.float32),
            pltpu.SemaphoreType.DMA((8, max(dp, loop))),
        ],
        compiler_params=pltpu.CompilerParams(
            collective_id=1, has_side_effects=True, vmem_limit_bytes=32 * 1024 * 1024
        ),
    )(part.reshape(dp, loop, rows, LANES))
    return summed.reshape(part.shape)


def dense_rows(values):
    return values.reshape(-1, LANES)


def on_device(
    features,
    image_ids,
    text_embeds,
    text_ids,
    depth_kernel,
    depth_bias,
    norm_gain,
    w_up,
    w_down,
    projection,
    logit_scale,
    logit_bias,
):
    image_rows = features.shape[0]
    channels = features.shape[3]
    hidden_share = w_up.shape[1]
    cell_count = GRID * GRID
    loop_count = lax.axis_size("loop")
    position = lax.axis_index("loop")
    image_count = image_rows * loop_count
    text_rows = text_embeds.shape[0]
    first_image = position * image_rows
    gather = functools.partial(lax.all_gather, axis_name="loop", axis=0, tiled=True)

    text_unit, text_inverse = unit_rows(text_embeds.astype(jnp.float32))
    cell_mean = jnp.mean(features.astype(jnp.float32), axis=(1, 2))

    padded = jnp.pad(
        features.astype(jnp.float32), ((0, 0), (0, 0), (0, ROWS - GRID), (0, 0))
    )
    gain_row = norm_gain[None, :]
    unit, inverse = conv_norm(
        padded,
        depth_kernel.astype(jnp.float32).reshape(cell_count, channels),
        depth_bias[None, :],
    )
    padded_rows = image_rows * GRID * ROWS
    unit_rows_own = unit.reshape(padded_rows, channels)
    unit_share = lax.all_to_all(unit_rows_own, "loop", split_axis=1, concat_axis=0, tiled=True)
    normed_rows = (unit_rows_own * gain_row).astype(jnp.bfloat16)
    pre_act = jnp.dot(normed_rows, w_up, preferred_element_type=jnp.float32)
    hidden_sum = jnp.sum(
        gelu_value(pre_act).reshape(image_rows, GRID * ROWS, hidden_share), axis=1
    )
    slope = gelu_slope(pre_act)
    slope_all = gather(slope)
    hidden_own = (hidden_sum / cell_count).astype(jnp.bfloat16)
    mlp_part = lax.dot_general(
        hidden_own, w_down, (((1,), (1,)), ((), ())), preferred_element_type=jnp.float32
    )
    id_row = jnp.pad(image_ids.astype(jnp.float32), (0, LANES - image_rows))[None, :]
    rest = jnp.concatenate([dense_rows(hidden_sum), dense_rows(text_unit), id_row], axis=0)
    hidden_rows = image_rows * hidden_share // LANES
    text_end = hidden_rows + text_unit.size // LANES
    rest = jnp.pad(rest, ((0, -rest.shape[0] % ROWS), (0, 0)))
    pooled_all, rest_all = head_exchange(dense_rows(mlp_part), dense_rows(cell_mean), rest)
    pooled = pooled_all.reshape(image_count, channels).astype(jnp.bfloat16)
    hidden_all = rest_all[:, :hidden_rows].reshape(image_count, hidden_share)
    hidden_all = (hidden_all / cell_count).astype(jnp.bfloat16)
    text_all = rest_all[:, hidden_rows:text_end].reshape(-1, text_embeds.shape[1])
    ids_all = rest_all[:, text_end, :image_rows].reshape(image_count).astype(jnp.int32)
    embedding = jnp.dot(pooled, projection, preferred_element_type=jnp.float32)
    image_unit, image_inverse = unit_rows(embedding)
    logits = (
        logit_scale[0] * jnp.dot(image_unit, text_all.T, precision=full_precision)
        + logit_bias[0]
    )
    labels = jnp.where(ids_all[:, None] == text_ids[None, :], 1.0, -1.0).astype(jnp.float32)
    loss_all = -jnp.sum(jax.nn.log_sigmoid(labels * logits), axis=1)
    row_loss = lax.dynamic_slice_in_dim(loss_all, first_image, image_rows)
    coeffs = -logit_scale[0] * labels * jax.nn.sigmoid(-labels * logits)
    grad_image = jnp.dot(coeffs, text_all, precision=full_precision)
    own_coeffs = lax.dynamic_slice_in_dim(coeffs, position * text_rows, text_rows, 1)
    grad_text = jnp.dot(own_coeffs.T, image_unit, precision=full_precision)
    grad_texts = text_inverse * (
        grad_text - text_unit * jnp.sum(text_unit * grad_text, axis=1, keepdims=True)
    )
    grad_embed = (
        image_inverse
        * (grad_image - image_unit * jnp.sum(image_unit * grad_image, axis=1, keepdims=True))
    ).astype(jnp.bfloat16)
    grad_pooled = lax.dot_general(
        grad_embed, projection, (((1,), (1,)), ((), ())), preferred_element_type=jnp.float32
    ).astype(jnp.bfloat16)
    spread = jnp.dot(grad_pooled, w_down, preferred_element_type=jnp.float32) / cell_count
    own_spread = lax.dynamic_slice_in_dim(spread, first_image, image_rows)
    grad_pre = (
        (slope.reshape(image_rows, GRID * ROWS, hidden_share) * own_spread[:, None, :])
        .reshape(padded_rows, hidden_share)
        .astype(jnp.bfloat16)
    )
    grad_normed = lax.dot_general(
        grad_pre, w_up, (((1,), (1,)), ((), ())), preferred_element_type=jnp.float32
    ).reshape(padded.shape)
    part = conv_grads(padded, unit, inverse, gain_row, grad_normed)
    total = total_sum(part).transpose(1, 0, 2).reshape(TAP_ROWS, channels)
    grad_kernel = total[:cell_count].reshape(GRID, GRID, channels)
    grad_bias = total[cell_count]
    grad_gain = total[cell_count + 1]

    up_share = channels // loop_count
    grad_pooled_share = lax.dynamic_slice_in_dim(grad_pooled, position * up_share, up_share, 1)
    grad_down = lax.dot_general(
        grad_pooled_share, hidden_all, (((0,), (0,)), ((), ())), preferred_element_type=jnp.float32
    )
    proj_share = up_share // lax.axis_size("dp")
    proj_at = (lax.axis_index("dp") * loop_count + position) * proj_share
    pooled_share = lax.dynamic_slice_in_dim(pooled, proj_at, proj_share, 1)
    grad_proj = lax.dot_general(
        pooled_share, grad_embed, (((0,), (0,)), ((), ())), preferred_element_type=jnp.float32
    )
    grad_pre_all = (
        (slope_all.reshape(image_count, GRID * ROWS, hidden_share) * spread[:, None, :])
        .reshape(loop_count * padded_rows, hidden_share)
        .astype(jnp.bfloat16)
    )
    gain_share = lax.dynamic_slice_in_dim(norm_gain, position * up_share, up_share)
    normed_share = (unit_share * gain_share).astype(jnp.bfloat16)
    grad_up = lax.dot_general(
        normed_share,
        grad_pre_all,
        (((0,), (0,)), ((), ())),
        preferred_element_type=jnp.float32,
    )
    return (row_loss, grad_texts, grad_kernel, grad_bias, grad_gain, grad_up, grad_down, grad_proj)


def solution(mesh):
    placed = (
        P("loop", None, None, None),
        P("loop"),
        P("loop", None),
        P(),
        P(),
        P(),
        P(),
        P(None, "dp"),
        P(None, "dp"),
        P(),
        P(),
        P(),
    )
    return jax.shard_map(
        on_device,
        mesh=mesh,
        in_specs=placed,
        out_specs=(
            P("loop"),
            P("loop", None),
            P(),
            P(),
            P(),
            P("loop", "dp"),
            P("loop", "dp"),
            P(("dp", "loop"), None),
        ),
        check_vma=False,
    )
```

```python
import functools
import jax
import jax.numpy as jnp
from jax import lax
from jax.experimental import pallas as pl
from jax.experimental.pallas import tpu as pltpu
from jax.sharding import PartitionSpec as P

GRID = 7
LANES = 128
ROWS = 8
TAP_ROWS = 64

full_precision = lax.Precision.HIGHEST
half_root = 0.7071067811865476
density_factor = 0.3989422804014327


def gelu_value(values):
    return 0.5 * values * (1.0 + lax.erf(values * half_root))


def gelu_slope(values):
    cumulative = 0.5 * (1.0 + lax.erf(values * half_root))
    return cumulative + values * jnp.exp(-0.5 * values * values) * density_factor


def unit_rows(values):
    inverse = lax.rsqrt(jnp.sum(values * values, axis=1, keepdims=True) + 1e-06)
    return (values * inverse, inverse)


def lane_tile(index):
    return pl.ds(pl.multiple_of(index * LANES, LANES), LANES)


def shifted_rows(x_ref, lanes, by, cell):
    count = x_ref.shape[0]
    moved = []
    for row in range(GRID):
        per_image = []
        for n in range(count):
            tile = x_ref[n, row, :, lanes]
            if by != 0:
                tile = pltpu.roll(tile, (-by) % ROWS, 0)
            if abs(by) > 1:
                inside = (cell + by >= 0) & (cell + by < GRID)
                tile = jnp.where(inside, tile, 0.0)
            per_image.append(tile)
        moved.append(per_image)
    return moved


def conv_norm_kernel(x_ref, k_ref, bias_ref, unit_ref, inv_ref):
    count = x_ref.shape[0]
    channels = x_ref.shape[3]
    tiles = channels // LANES
    reach = (GRID - 1) // 2
    cell = lax.broadcasted_iota(jnp.int32, (ROWS, LANES), 0)
    cells = [(n, p) for p in range(GRID) for n in range(count)]

    def conv_tile(index, sums):
        lanes = lane_tile(index)
        bias = jnp.broadcast_to(bias_ref[:, lanes], (ROWS, LANES))
        out = {at: bias for at in cells}
        for col_off in range(GRID):
            moved = shifted_rows(x_ref, lanes, col_off - reach, cell)
            for row_off in range(GRID):
                tap = row_off * GRID + col_off
                weight = jnp.broadcast_to(k_ref[tap : tap + 1, lanes], (ROWS, LANES))
                for p in range(GRID):
                    row = p + row_off - reach
                    if 0 <= row < GRID:
                        for n in range(count):
                            out[(n, p)] = out[(n, p)] + moved[row][n] * weight
        for n, p in cells:
            unit_ref[n, p, :, lanes] = out[(n, p)]
        return tuple(total + out[at] for total, at in zip(sums, cells))

    zeros = tuple(jnp.zeros((ROWS, LANES), jnp.float32) for _ in cells)
    sums = lax.fori_loop(0, tiles, conv_tile, zeros)
    means = [jnp.sum(total, axis=1, keepdims=True) / channels for total in sums]
    means = [jnp.broadcast_to(mean, (ROWS, LANES)) for mean in means]

    def square_tile(index, sums):
        lanes = lane_tile(index)
        result = []
        for total, mean, (n, p) in zip(sums, means, cells):
            centered = unit_ref[n, p, :, lanes] - mean
            result.append(total + centered * centered)
        return tuple(result)

    squares = lax.fori_loop(0, tiles, square_tile, zeros)
    inverses = []
    for total, (n, p) in zip(squares, cells):
        variance = jnp.sum(total, axis=1, keepdims=True) / channels
        inverse = jnp.broadcast_to(lax.rsqrt(variance + 1e-06), (ROWS, LANES))
        inverse = jnp.where(cell < GRID, inverse, 0.0)
        inv_ref[n, p, :, :] = inverse
        inverses.append(inverse)

    def norm_tile(index, carry):
        lanes = lane_tile(index)
        for inverse, mean, (n, p) in zip(inverses, means, cells):
            unit = (unit_ref[n, p, :, lanes] - mean) * inverse
            unit_ref[n, p, :, lanes] = unit
        return carry

    lax.fori_loop(0, tiles, norm_tile, 0)


def conv_norm(padded, taps, bias):
    count, _, _, channels = padded.shape
    whole = pl.BlockSpec(memory_space=pltpu.VMEM)
    full = jax.ShapeDtypeStruct(padded.shape, jnp.float32)
    return pl.pallas_call(
        conv_norm_kernel,
        out_shape=(
            full,
            jax.ShapeDtypeStruct((count, GRID, ROWS, LANES), jnp.float32),
        ),
        in_specs=[whole] * 3,
        out_specs=(whole, whole),
        compiler_params=pltpu.CompilerParams(vmem_limit_bytes=24 * 1024 * 1024),
    )(padded, taps, bias)


def conv_grad_kernel(x_ref, unit_ref, inv_ref, gain_ref, grad_ref, out_ref, work_ref):
    count = x_ref.shape[0]
    channels = x_ref.shape[3]
    tiles = channels // LANES
    reach = (GRID - 1) // 2
    taps = GRID * GRID
    cell = lax.broadcasted_iota(jnp.int32, (ROWS, LANES), 0)
    cells = [(n, p) for p in range(GRID) for n in range(count)]
    zero = jnp.zeros((ROWS, LANES), jnp.float32)

    def first_tile(index, carry):
        plain, crossed = carry
        lanes = lane_tile(index)
        gain = jnp.broadcast_to(gain_ref[:, lanes], (ROWS, LANES))
        gain_sum = zero
        out_ref[index, 48:TAP_ROWS, :] = jnp.zeros((TAP_ROWS - 48, LANES), jnp.float32)
        plain_out = []
        crossed_out = []
        for at, (n, p) in enumerate(cells):
            unit = unit_ref[n, p, :, lanes]
            grad = grad_ref[n, p, :, lanes]
            gain_sum = gain_sum + grad * unit
            scaled = grad * gain
            plain_out.append(plain[at] + scaled)
            crossed_out.append(crossed[at] + scaled * unit)
        out_ref[index, taps + 1 : taps + 2, :] = jnp.sum(gain_sum, axis=0, keepdims=True)
        return (tuple(plain_out), tuple(crossed_out))

    zeros = tuple(zero for _ in cells)
    plain, crossed = lax.fori_loop(0, tiles, first_tile, (zeros, zeros))
    for at, (n, p) in enumerate(cells):
        first = jnp.sum(plain[at], axis=1, keepdims=True) / channels
        second = jnp.sum(crossed[at], axis=1, keepdims=True) / channels
        work_ref[0, n, p, :, :] = jnp.broadcast_to(first, (ROWS, LANES))
        work_ref[1, n, p, :, :] = jnp.broadcast_to(second, (ROWS, LANES))

    def tap_tile(index, carry):
        lanes = lane_tile(index)
        gain = jnp.broadcast_to(gain_ref[:, lanes], (ROWS, LANES))
        grad_conv = {}
        bias_sum = zero
        for n, p in cells:
            value = inv_ref[n, p, :, :] * (
                grad_ref[n, p, :, lanes] * gain
                - work_ref[0, n, p, :, :]
                - unit_ref[n, p, :, lanes] * work_ref[1, n, p, :, :]
            )
            grad_conv[(n, p)] = value
            bias_sum = bias_sum + value
        out_ref[index, taps : taps + 1, :] = jnp.sum(bias_sum, axis=0, keepdims=True)
        for col_off in range(GRID):
            moved = shifted_rows(x_ref, lanes, col_off - reach, cell)
            for row_off in range(GRID):
                tap = row_off * GRID + col_off
                total = zero
                for p in range(GRID):
                    row = p + row_off - reach
                    if 0 <= row < GRID:
                        for n in range(count):
                            total = total + moved[row][n] * grad_conv[(n, p)]
                out_ref[index, tap : tap + 1, :] = jnp.sum(total, axis=0, keepdims=True)
        return carry

    lax.fori_loop(0, tiles, tap_tile, 0)


def conv_grads(padded, unit, inverse, gain, grad):
    count, _, _, channels = padded.shape
    whole = pl.BlockSpec(memory_space=pltpu.VMEM)
    return pl.pallas_call(
        conv_grad_kernel,
        out_shape=jax.ShapeDtypeStruct((channels // LANES, TAP_ROWS, LANES), jnp.float32),
        in_specs=[whole] * 5,
        out_specs=whole,
        scratch_shapes=[pltpu.VMEM((2, count, GRID, ROWS, LANES), jnp.float32)],
        compiler_params=pltpu.CompilerParams(vmem_limit_bytes=24 * 1024 * 1024),
    )(padded, unit, inverse, gain, grad)


def peer_copies(axis, count, source_of, target, send_sems, recv_sems):
    me = lax.axis_index(axis)
    copies = []
    for by in range(1, count):
        peer = lax.rem(me + by, count)
        copy = pltpu.make_async_remote_copy(
            src_ref=source_of(peer),
            dst_ref=target.at[me],
            send_sem=send_sems.at[by],
            recv_sem=recv_sems.at[by],
            device_id={axis: peer},
            device_id_type=pl.DeviceIdType.MESH,
        )
        copy.start()
        copies.append(copy)
    return copies


def wait_all(copies):
    for copy in copies:
        copy.wait()


def meet_peers(sizes):
    barrier = pltpu.get_barrier_semaphore()
    total = 0
    for axis, count in sizes:
        me = lax.axis_index(axis)
        for by in range(1, count):
            pl.semaphore_signal(
                barrier,
                inc=1,
                device_id={axis: lax.rem(me + by, count)},
                device_id_type=pl.DeviceIdType.MESH,
            )
        total += count - 1
    pl.semaphore_wait(barrier, total)


def head_kernel(
    dp, loop, part_ref, mean_ref, rest_ref, pooled_ref, rest_out_ref, parts, own, sems
):
    meet_peers((("dp", dp), ("loop", loop)))
    loop_me = lax.axis_index("loop")
    dp_me = lax.axis_index("dp")
    dp_copies = peer_copies(
        "dp", dp, lambda peer: part_ref, parts, sems.at[0], sems.at[1]
    )
    rest_copies = peer_copies(
        "loop", loop, lambda peer: rest_ref, rest_out_ref, sems.at[2], sems.at[3]
    )
    parts[dp_me] = part_ref[...]
    rest_out_ref[loop_me] = rest_ref[...]
    wait_all(dp_copies)
    total = parts[0]
    for at in range(1, dp):
        total = total + parts[at]
    own[...] = mean_ref[...] + total
    pooled_copies = peer_copies(
        "loop", loop, lambda peer: own, pooled_ref, sems.at[4], sems.at[5]
    )
    pooled_ref[loop_me] = own[...]
    wait_all(rest_copies)
    wait_all(pooled_copies)


def head_exchange(part, mean, rest):
    dp = lax.axis_size("dp")
    loop = lax.axis_size("loop")
    whole = pl.BlockSpec(memory_space=pltpu.VMEM)
    return pl.pallas_call(
        functools.partial(head_kernel, dp, loop),
        out_shape=(
            jax.ShapeDtypeStruct((loop,) + part.shape, jnp.float32),
            jax.ShapeDtypeStruct((loop,) + rest.shape, jnp.float32),
        ),
        in_specs=[whole] * 3,
        out_specs=(whole, whole),
        scratch_shapes=[
            pltpu.VMEM((dp,) + part.shape, jnp.float32),
            pltpu.VMEM(part.shape, jnp.float32),
            pltpu.SemaphoreType.DMA((6, max(dp, loop))),
        ],
        cost_estimate=pl.CostEstimate(flops=1000, bytes_accessed=1000, transcendentals=0),
        compiler_params=pltpu.CompilerParams(
            collective_id=0, has_side_effects=True, vmem_limit_bytes=16 * 1024 * 1024
        ),
    )(part, mean, rest)


def total_kernel(dp, loop, part_ref, out_ref, dp_slots, loop_slots, block, chunk, sems):
    meet_peers((("dp", dp), ("loop", loop)))
    loop_me = lax.axis_index("loop")
    dp_me = lax.axis_index("dp")
    copies = peer_copies(
        "dp", dp, lambda peer: part_ref.at[peer], dp_slots, sems.at[0], sems.at[1]
    )
    dp_slots[dp_me] = part_ref[dp_me]
    wait_all(copies)
    total = dp_slots[0]
    for at in range(1, dp):
        total = total + dp_slots[at]
    block[...] = total
    copies = peer_copies(
        "loop", loop, lambda peer: block.at[peer], loop_slots, sems.at[2], sems.at[3]
    )
    loop_slots[loop_me] = block[loop_me]
    wait_all(copies)
    total = loop_slots[0]
    for at in range(1, loop):
        total = total + loop_slots[at]
    chunk[...] = total
    mine = out_ref.at[dp_me]
    copies = peer_copies("loop", loop, lambda peer: chunk, mine, sems.at[4], sems.at[5])
    out_ref[dp_me, loop_me] = chunk[...]
    wait_all(copies)
    copies = peer_copies("dp", dp, lambda peer: mine, out_ref, sems.at[6], sems.at[7])
    wait_all(copies)


def total_sum(part):
    dp = lax.axis_size("dp")
    loop = lax.axis_size("loop")
    rows = part.shape[0] * part.shape[1] // (dp * loop)
    whole = pl.BlockSpec(memory_space=pltpu.VMEM)
    summed = pl.pallas_call(
        functools.partial(total_kernel, dp, loop),
        out_shape=jax.ShapeDtypeStruct((dp, loop, rows, LANES), jnp.float32),
        in_specs=[whole],
        out_specs=whole,
        scratch_shapes=[
            pltpu.VMEM((dp, loop, rows, LANES), jnp.float32),
            pltpu.VMEM((loop, rows, LANES), jnp.float32),
            pltpu.VMEM((loop, rows, LANES), jnp.float32),
            pltpu.VMEM((rows, LANES), jnp.float32),
            pltpu.SemaphoreType.DMA((8, max(dp, loop))),
        ],
        compiler_params=pltpu.CompilerParams(
            collective_id=1, has_side_effects=True, vmem_limit_bytes=32 * 1024 * 1024
        ),
    )(part.reshape(dp, loop, rows, LANES))
    return summed.reshape(part.shape)


def dense_rows(values):
    return values.reshape(-1, LANES)


def on_device(
    features,
    image_ids,
    text_embeds,
    text_ids,
    depth_kernel,
    depth_bias,
    norm_gain,
    w_up,
    w_down,
    projection,
    logit_scale,
    logit_bias,
):
    image_rows = features.shape[0]
    channels = features.shape[3]
    hidden_share = w_up.shape[1]
    cell_count = GRID * GRID
    loop_count = lax.axis_size("loop")
    position = lax.axis_index("loop")
    image_count = image_rows * loop_count
    text_rows = text_embeds.shape[0]
    first_image = position * image_rows
    gather = functools.partial(lax.all_gather, axis_name="loop", axis=0, tiled=True)

    text_unit, text_inverse = unit_rows(text_embeds.astype(jnp.float32))
    cell_mean = jnp.mean(features.astype(jnp.float32), axis=(1, 2))

    padded = jnp.pad(
        features.astype(jnp.float32), ((0, 0), (0, 0), (0, ROWS - GRID), (0, 0))
    )
    gain_row = norm_gain[None, :]
    unit, inverse = conv_norm(
        padded,
        depth_kernel.astype(jnp.float32).reshape(cell_count, channels),
        depth_bias[None, :],
    )
    padded_rows = image_rows * GRID * ROWS
    unit_rows_own = unit.reshape(padded_rows, channels)
    unit_share = lax.all_to_all(unit_rows_own, "loop", split_axis=1, concat_axis=0, tiled=True)
    normed_rows = (unit_rows_own * gain_row).astype(jnp.bfloat16)
    pre_act = jnp.dot(normed_rows, w_up, preferred_element_type=jnp.float32)
    hidden_sum = jnp.sum(
        gelu_value(pre_act).reshape(image_rows, GRID * ROWS, hidden_share), axis=1
    )
    slope = gelu_slope(pre_act)
    slope_all = gather(slope)
    hidden_own = (hidden_sum / cell_count).astype(jnp.bfloat16)
    mlp_part = lax.dot_general(
        hidden_own, w_down, (((1,), (1,)), ((), ())), preferred_element_type=jnp.float32
    )
    id_row = jnp.pad(image_ids.astype(jnp.float32), (0, LANES - image_rows))[None, :]
    rest = jnp.concatenate([dense_rows(hidden_sum), dense_rows(text_unit), id_row], axis=0)
    hidden_rows = image_rows * hidden_share // LANES
    text_end = hidden_rows + text_unit.size // LANES
    rest = jnp.pad(rest, ((0, -rest.shape[0] % ROWS), (0, 0)))
    pooled_all, rest_all = head_exchange(dense_rows(mlp_part), dense_rows(cell_mean), rest)
    pooled = pooled_all.reshape(image_count, channels).astype(jnp.bfloat16)
    hidden_all = rest_all[:, :hidden_rows].reshape(image_count, hidden_share)
    hidden_all = (hidden_all / cell_count).astype(jnp.bfloat16)
    text_all = rest_all[:, hidden_rows:text_end].reshape(-1, text_embeds.shape[1])
    ids_all = rest_all[:, text_end, :image_rows].reshape(image_count).astype(jnp.int32)
    embedding = jnp.dot(pooled, projection, preferred_element_type=jnp.float32)
    image_unit, image_inverse = unit_rows(embedding)
    logits = (
        logit_scale[0] * jnp.dot(image_unit, text_all.T, precision=full_precision)
        + logit_bias[0]
    )
    labels = jnp.where(ids_all[:, None] == text_ids[None, :], 1.0, -1.0).astype(jnp.float32)
    loss_all = -jnp.sum(jax.nn.log_sigmoid(labels * logits), axis=1)
    row_loss = lax.dynamic_slice_in_dim(loss_all, first_image, image_rows)
    coeffs = -logit_scale[0] * labels * jax.nn.sigmoid(-labels * logits)
    grad_image = jnp.dot(coeffs, text_all, precision=full_precision)
    own_coeffs = lax.dynamic_slice_in_dim(coeffs, position * text_rows, text_rows, 1)
    grad_text = jnp.dot(own_coeffs.T, image_unit, precision=full_precision)
    grad_texts = text_inverse * (
        grad_text - text_unit * jnp.sum(text_unit * grad_text, axis=1, keepdims=True)
    )
    grad_embed = (
        image_inverse
        * (grad_image - image_unit * jnp.sum(image_unit * grad_image, axis=1, keepdims=True))
    ).astype(jnp.bfloat16)
    grad_pooled = lax.dot_general(
        grad_embed, projection, (((1,), (1,)), ((), ())), preferred_element_type=jnp.float32
    ).astype(jnp.bfloat16)
    spread = jnp.dot(grad_pooled, w_down, preferred_element_type=jnp.float32) / cell_count
    spread, slope_all, unit_share = lax.optimization_barrier((spread, slope_all, unit_share))
    own_spread = lax.dynamic_slice_in_dim(spread, first_image, image_rows)
    grad_pre = (
        (slope.reshape(image_rows, GRID * ROWS, hidden_share) * own_spread[:, None, :])
        .reshape(padded_rows, hidden_share)
        .astype(jnp.bfloat16)
    )
    grad_normed = lax.dot_general(
        grad_pre, w_up, (((1,), (1,)), ((), ())), preferred_element_type=jnp.float32
    ).reshape(padded.shape)
    part = conv_grads(padded, unit, inverse, gain_row, grad_normed)
    total = total_sum(part).transpose(1, 0, 2).reshape(TAP_ROWS, channels)
    grad_kernel = total[:cell_count].reshape(GRID, GRID, channels)
    grad_bias = total[cell_count]
    grad_gain = total[cell_count + 1]

    up_share = channels // loop_count
    grad_pooled_share = lax.dynamic_slice_in_dim(grad_pooled, position * up_share, up_share, 1)
    grad_down = lax.dot_general(
        grad_pooled_share, hidden_all, (((0,), (0,)), ((), ())), preferred_element_type=jnp.float32
    )
    proj_share = up_share // lax.axis_size("dp")
    proj_at = (lax.axis_index("dp") * loop_count + position) * proj_share
    pooled_share = lax.dynamic_slice_in_dim(pooled, proj_at, proj_share, 1)
    grad_proj = lax.dot_general(
        pooled_share, grad_embed, (((0,), (0,)), ((), ())), preferred_element_type=jnp.float32
    )
    grad_pre_all = (
        (slope_all.reshape(image_count, GRID * ROWS, hidden_share) * spread[:, None, :])
        .reshape(loop_count * padded_rows, hidden_share)
        .astype(jnp.bfloat16)
    )
    gain_share = lax.dynamic_slice_in_dim(norm_gain, position * up_share, up_share)
    normed_share = (unit_share * gain_share).astype(jnp.bfloat16)
    grad_up = lax.dot_general(
        normed_share,
        grad_pre_all,
        (((0,), (0,)), ((), ())),
        preferred_element_type=jnp.float32,
    )
    return (row_loss, grad_texts, grad_kernel, grad_bias, grad_gain, grad_up, grad_down, grad_proj)


def solution(mesh):
    placed = (
        P("loop", None, None, None),
        P("loop"),
        P("loop", None),
        P(),
        P(),
        P(),
        P(),
        P(None, "dp"),
        P(None, "dp"),
        P(),
        P(),
        P(),
    )
    return jax.shard_map(
        on_device,
        mesh=mesh,
        in_specs=placed,
        out_specs=(
            P("loop"),
            P("loop", None),
            P(),
            P(),
            P(),
            P("loop", "dp"),
            P("loop", "dp"),
            P(("dp", "loop"), None),
        ),
        check_vma=False,
    )
```

```python
import functools
import jax
import jax.numpy as jnp
from jax import lax
from jax.experimental import pallas as pl
from jax.experimental.pallas import tpu as pltpu
from jax.sharding import PartitionSpec as P

GRID = 7
LANES = 128
ROWS = 8
TAP_ROWS = 64

full_precision = lax.Precision.HIGHEST
half_root = 0.7071067811865476
density_factor = 0.3989422804014327


def gelu_value(values):
    return 0.5 * values * (1.0 + lax.erf(values * half_root))


def gelu_slope(values):
    cumulative = 0.5 * (1.0 + lax.erf(values * half_root))
    return cumulative + values * jnp.exp(-0.5 * values * values) * density_factor


def unit_rows(values):
    inverse = lax.rsqrt(jnp.sum(values * values, axis=1, keepdims=True) + 1e-06)
    return (values * inverse, inverse)


def lane_tile(index):
    return pl.ds(pl.multiple_of(index * LANES, LANES), LANES)


def shifted_rows(x_ref, lanes, by, cell):
    count = x_ref.shape[0]
    moved = []
    for row in range(GRID):
        per_image = []
        for n in range(count):
            tile = x_ref[n, row, :, lanes]
            if by != 0:
                tile = pltpu.roll(tile, (-by) % ROWS, 0)
            if abs(by) > 1:
                inside = (cell + by >= 0) & (cell + by < GRID)
                tile = jnp.where(inside, tile, 0.0)
            per_image.append(tile)
        moved.append(per_image)
    return moved


def conv_norm_kernel(x_ref, k_ref, bias_ref, unit_ref, inv_ref):
    count = x_ref.shape[0]
    channels = x_ref.shape[3]
    tiles = channels // LANES
    reach = (GRID - 1) // 2
    cell = lax.broadcasted_iota(jnp.int32, (ROWS, LANES), 0)
    cells = [(n, p) for p in range(GRID) for n in range(count)]

    def conv_tile(index, sums):
        lanes = lane_tile(index)
        bias = jnp.broadcast_to(bias_ref[:, lanes], (ROWS, LANES))
        out = {at: bias for at in cells}
        for col_off in range(GRID):
            moved = shifted_rows(x_ref, lanes, col_off - reach, cell)
            for row_off in range(GRID):
                tap = row_off * GRID + col_off
                weight = jnp.broadcast_to(k_ref[tap : tap + 1, lanes], (ROWS, LANES))
                for p in range(GRID):
                    row = p + row_off - reach
                    if 0 <= row < GRID:
                        for n in range(count):
                            out[(n, p)] = out[(n, p)] + moved[row][n] * weight
        for n, p in cells:
            unit_ref[n, p, :, lanes] = out[(n, p)]
        return tuple(total + out[at] for total, at in zip(sums, cells))

    zeros = tuple(jnp.zeros((ROWS, LANES), jnp.float32) for _ in cells)
    sums = lax.fori_loop(0, tiles, conv_tile, zeros)
    means = [jnp.sum(total, axis=1, keepdims=True) / channels for total in sums]
    means = [jnp.broadcast_to(mean, (ROWS, LANES)) for mean in means]

    def square_tile(index, sums):
        lanes = lane_tile(index)
        result = []
        for total, mean, (n, p) in zip(sums, means, cells):
            centered = unit_ref[n, p, :, lanes] - mean
            result.append(total + centered * centered)
        return tuple(result)

    squares = lax.fori_loop(0, tiles, square_tile, zeros)
    inverses = []
    for total, (n, p) in zip(squares, cells):
        variance = jnp.sum(total, axis=1, keepdims=True) / channels
        inverse = jnp.broadcast_to(lax.rsqrt(variance + 1e-06), (ROWS, LANES))
        inverse = jnp.where(cell < GRID, inverse, 0.0)
        inv_ref[n, p, :, :] = inverse
        inverses.append(inverse)

    def norm_tile(index, carry):
        lanes = lane_tile(index)
        for inverse, mean, (n, p) in zip(inverses, means, cells):
            unit = (unit_ref[n, p, :, lanes] - mean) * inverse
            unit_ref[n, p, :, lanes] = unit
        return carry

    lax.fori_loop(0, tiles, norm_tile, 0)


def conv_norm(padded, taps, bias):
    count, _, _, channels = padded.shape
    whole = pl.BlockSpec(memory_space=pltpu.VMEM)
    full = jax.ShapeDtypeStruct(padded.shape, jnp.float32)
    return pl.pallas_call(
        conv_norm_kernel,
        out_shape=(
            full,
            jax.ShapeDtypeStruct((count, GRID, ROWS, LANES), jnp.float32),
        ),
        in_specs=[whole] * 3,
        out_specs=(whole, whole),
        compiler_params=pltpu.CompilerParams(vmem_limit_bytes=24 * 1024 * 1024),
    )(padded, taps, bias)


def conv_grad_kernel(x_ref, unit_ref, inv_ref, gain_ref, grad_ref, out_ref, work_ref):
    count = x_ref.shape[0]
    channels = x_ref.shape[3]
    tiles = channels // LANES
    reach = (GRID - 1) // 2
    taps = GRID * GRID
    cell = lax.broadcasted_iota(jnp.int32, (ROWS, LANES), 0)
    cells = [(n, p) for p in range(GRID) for n in range(count)]
    zero = jnp.zeros((ROWS, LANES), jnp.float32)

    def first_tile(index, carry):
        plain, crossed = carry
        lanes = lane_tile(index)
        gain = jnp.broadcast_to(gain_ref[:, lanes], (ROWS, LANES))
        gain_sum = zero
        out_ref[index, 48:TAP_ROWS, :] = jnp.zeros((TAP_ROWS - 48, LANES), jnp.float32)
        plain_out = []
        crossed_out = []
        for at, (n, p) in enumerate(cells):
            unit = unit_ref[n, p, :, lanes]
            grad = grad_ref[n, p, :, lanes]
            gain_sum = gain_sum + grad * unit
            scaled = grad * gain
            plain_out.append(plain[at] + scaled)
            crossed_out.append(crossed[at] + scaled * unit)
        out_ref[index, taps + 1 : taps + 2, :] = jnp.sum(gain_sum, axis=0, keepdims=True)
        return (tuple(plain_out), tuple(crossed_out))

    zeros = tuple(zero for _ in cells)
    plain, crossed = lax.fori_loop(0, tiles, first_tile, (zeros, zeros))
    for at, (n, p) in enumerate(cells):
        first = jnp.sum(plain[at], axis=1, keepdims=True) / channels
        second = jnp.sum(crossed[at], axis=1, keepdims=True) / channels
        work_ref[0, n, p, :, :] = jnp.broadcast_to(first, (ROWS, LANES))
        work_ref[1, n, p, :, :] = jnp.broadcast_to(second, (ROWS, LANES))

    def tap_tile(index, carry):
        lanes = lane_tile(index)
        gain = jnp.broadcast_to(gain_ref[:, lanes], (ROWS, LANES))
        grad_conv = {}
        bias_sum = zero
        for n, p in cells:
            value = inv_ref[n, p, :, :] * (
                grad_ref[n, p, :, lanes] * gain
                - work_ref[0, n, p, :, :]
                - unit_ref[n, p, :, lanes] * work_ref[1, n, p, :, :]
            )
            grad_conv[(n, p)] = value
            bias_sum = bias_sum + value
        out_ref[index, taps : taps + 1, :] = jnp.sum(bias_sum, axis=0, keepdims=True)
        for col_off in range(GRID):
            moved = shifted_rows(x_ref, lanes, col_off - reach, cell)
            for row_off in range(GRID):
                tap = row_off * GRID + col_off
                total = zero
                for p in range(GRID):
                    row = p + row_off - reach
                    if 0 <= row < GRID:
                        for n in range(count):
                            total = total + moved[row][n] * grad_conv[(n, p)]
                out_ref[index, tap : tap + 1, :] = jnp.sum(total, axis=0, keepdims=True)
        return carry

    lax.fori_loop(0, tiles, tap_tile, 0)


def conv_grads(padded, unit, inverse, gain, grad):
    count, _, _, channels = padded.shape
    whole = pl.BlockSpec(memory_space=pltpu.VMEM)
    return pl.pallas_call(
        conv_grad_kernel,
        out_shape=jax.ShapeDtypeStruct((channels // LANES, TAP_ROWS, LANES), jnp.float32),
        in_specs=[whole] * 5,
        out_specs=whole,
        scratch_shapes=[pltpu.VMEM((2, count, GRID, ROWS, LANES), jnp.float32)],
        compiler_params=pltpu.CompilerParams(vmem_limit_bytes=24 * 1024 * 1024),
    )(padded, unit, inverse, gain, grad)


def peer_copies(axis, count, source_of, target, send_sems, recv_sems):
    me = lax.axis_index(axis)
    copies = []
    for by in range(1, count):
        peer = lax.rem(me + by, count)
        copy = pltpu.make_async_remote_copy(
            src_ref=source_of(peer),
            dst_ref=target.at[me],
            send_sem=send_sems.at[by],
            recv_sem=recv_sems.at[by],
            device_id={axis: peer},
            device_id_type=pl.DeviceIdType.MESH,
        )
        copy.start()
        copies.append(copy)
    return copies


def wait_all(copies):
    for copy in copies:
        copy.wait()


def meet_peers(sizes):
    barrier = pltpu.get_barrier_semaphore()
    total = 0
    for axis, count in sizes:
        me = lax.axis_index(axis)
        for by in range(1, count):
            pl.semaphore_signal(
                barrier,
                inc=1,
                device_id={axis: lax.rem(me + by, count)},
                device_id_type=pl.DeviceIdType.MESH,
            )
        total += count - 1
    pl.semaphore_wait(barrier, total)


def head_kernel(
    dp, loop, part_ref, mean_ref, rest_ref, pooled_ref, rest_out_ref, parts, own, sems
):
    meet_peers((("dp", dp), ("loop", loop)))
    loop_me = lax.axis_index("loop")
    dp_me = lax.axis_index("dp")
    dp_copies = peer_copies(
        "dp", dp, lambda peer: part_ref, parts, sems.at[0], sems.at[1]
    )
    rest_copies = peer_copies(
        "loop", loop, lambda peer: rest_ref, rest_out_ref, sems.at[2], sems.at[3]
    )
    parts[dp_me] = part_ref[...]
    rest_out_ref[loop_me] = rest_ref[...]
    wait_all(dp_copies)
    total = parts[0]
    for at in range(1, dp):
        total = total + parts[at]
    own[...] = mean_ref[...] + total
    pooled_copies = peer_copies(
        "loop", loop, lambda peer: own, pooled_ref, sems.at[4], sems.at[5]
    )
    pooled_ref[loop_me] = own[...]
    wait_all(rest_copies)
    wait_all(pooled_copies)


def head_exchange(part, mean, rest):
    dp = lax.axis_size("dp")
    loop = lax.axis_size("loop")
    whole = pl.BlockSpec(memory_space=pltpu.VMEM)
    return pl.pallas_call(
        functools.partial(head_kernel, dp, loop),
        out_shape=(
            jax.ShapeDtypeStruct((loop,) + part.shape, jnp.float32),
            jax.ShapeDtypeStruct((loop,) + rest.shape, jnp.float32),
        ),
        in_specs=[whole] * 3,
        out_specs=(whole, whole),
        scratch_shapes=[
            pltpu.VMEM((dp,) + part.shape, jnp.float32),
            pltpu.VMEM(part.shape, jnp.float32),
            pltpu.SemaphoreType.DMA((6, max(dp, loop))),
        ],
        compiler_params=pltpu.CompilerParams(
            collective_id=0, has_side_effects=True, vmem_limit_bytes=16 * 1024 * 1024
        ),
    )(part, mean, rest)


def total_kernel(dp, loop, part_ref, out_ref, dp_slots, loop_slots, block, chunk, sems):
    meet_peers((("dp", dp), ("loop", loop)))
    loop_me = lax.axis_index("loop")
    dp_me = lax.axis_index("dp")
    copies = peer_copies(
        "dp", dp, lambda peer: part_ref.at[peer], dp_slots, sems.at[0], sems.at[1]
    )
    dp_slots[dp_me] = part_ref[dp_me]
    wait_all(copies)
    total = dp_slots[0]
    for at in range(1, dp):
        total = total + dp_slots[at]
    block[...] = total
    copies = peer_copies(
        "loop", loop, lambda peer: block.at[peer], loop_slots, sems.at[2], sems.at[3]
    )
    loop_slots[loop_me] = block[loop_me]
    wait_all(copies)
    total = loop_slots[0]
    for at in range(1, loop):
        total = total + loop_slots[at]
    chunk[...] = total
    mine = out_ref.at[dp_me]
    copies = peer_copies("loop", loop, lambda peer: chunk, mine, sems.at[4], sems.at[5])
    out_ref[dp_me, loop_me] = chunk[...]
    wait_all(copies)
    copies = peer_copies("dp", dp, lambda peer: mine, out_ref, sems.at[6], sems.at[7])
    wait_all(copies)


def total_sum(part):
    dp = lax.axis_size("dp")
    loop = lax.axis_size("loop")
    rows = part.shape[0] * part.shape[1] // (dp * loop)
    whole = pl.BlockSpec(memory_space=pltpu.VMEM)
    summed = pl.pallas_call(
        functools.partial(total_kernel, dp, loop),
        out_shape=jax.ShapeDtypeStruct((dp, loop, rows, LANES), jnp.float32),
        in_specs=[whole],
        out_specs=whole,
        scratch_shapes=[
            pltpu.VMEM((dp, loop, rows, LANES), jnp.float32),
            pltpu.VMEM((loop, rows, LANES), jnp.float32),
            pltpu.VMEM((loop, rows, LANES), jnp.float32),
            pltpu.VMEM((rows, LANES), jnp.float32),
            pltpu.SemaphoreType.DMA((8, max(dp, loop))),
        ],
        compiler_params=pltpu.CompilerParams(
            collective_id=1, has_side_effects=True, vmem_limit_bytes=32 * 1024 * 1024
        ),
    )(part.reshape(dp, loop, rows, LANES))
    return summed.reshape(part.shape)


def dense_rows(values):
    return values.reshape(-1, LANES)


def on_device(
    features,
    image_ids,
    text_embeds,
    text_ids,
    depth_kernel,
    depth_bias,
    norm_gain,
    w_up,
    w_down,
    projection,
    logit_scale,
    logit_bias,
):
    image_rows = features.shape[0]
    channels = features.shape[3]
    hidden_share = w_up.shape[1]
    cell_count = GRID * GRID
    loop_count = lax.axis_size("loop")
    position = lax.axis_index("loop")
    image_count = image_rows * loop_count
    text_rows = text_embeds.shape[0]
    first_image = position * image_rows
    gather = functools.partial(lax.all_gather, axis_name="loop", axis=0, tiled=True)

    text_unit, text_inverse = unit_rows(text_embeds.astype(jnp.float32))
    cell_mean = jnp.mean(features.astype(jnp.float32), axis=(1, 2))

    padded = jnp.pad(
        features.astype(jnp.float32), ((0, 0), (0, 0), (0, ROWS - GRID), (0, 0))
    )
    gain_row = norm_gain[None, :]
    unit, inverse = conv_norm(
        padded,
        depth_kernel.astype(jnp.float32).reshape(cell_count, channels),
        depth_bias[None, :],
    )
    padded_rows = image_rows * GRID * ROWS
    unit_rows_own = unit.reshape(padded_rows, channels)
    unit_share = lax.all_to_all(unit_rows_own, "loop", split_axis=1, concat_axis=0, tiled=True)
    normed_rows = (unit_rows_own * gain_row).astype(jnp.bfloat16)
    pre_act = jnp.dot(normed_rows, w_up, preferred_element_type=jnp.float32)
    hidden_sum = jnp.sum(
        gelu_value(pre_act).reshape(image_rows, GRID * ROWS, hidden_share), axis=1
    )
    slope = gelu_slope(pre_act)
    hidden_own = (hidden_sum / cell_count).astype(jnp.bfloat16)
    mlp_part = lax.dot_general(
        hidden_own, w_down, (((1,), (1,)), ((), ())), preferred_element_type=jnp.float32
    )
    id_row = jnp.pad(image_ids.astype(jnp.float32), (0, LANES - image_rows))[None, :]
    rest = jnp.concatenate([dense_rows(hidden_sum), dense_rows(text_unit), id_row], axis=0)
    hidden_rows = image_rows * hidden_share // LANES
    text_end = hidden_rows + text_unit.size // LANES
    rest = jnp.pad(rest, ((0, -rest.shape[0] % ROWS), (0, 0)))
    pooled_all, rest_all = head_exchange(dense_rows(mlp_part), dense_rows(cell_mean), rest)
    slope_sent, unit_share, pooled_all = lax.optimization_barrier((slope, unit_share, pooled_all))
    slope_all = gather(slope_sent)
    pooled = pooled_all.reshape(image_count, channels).astype(jnp.bfloat16)
    hidden_all = rest_all[:, :hidden_rows].reshape(image_count, hidden_share)
    hidden_all = (hidden_all / cell_count).astype(jnp.bfloat16)
    text_all = rest_all[:, hidden_rows:text_end].reshape(-1, text_embeds.shape[1])
    ids_all = rest_all[:, text_end, :image_rows].reshape(image_count).astype(jnp.int32)
    embedding = jnp.dot(pooled, projection, preferred_element_type=jnp.float32)
    image_unit, image_inverse = unit_rows(embedding)
    logits = (
        logit_scale[0] * jnp.dot(image_unit, text_all.T, precision=full_precision)
        + logit_bias[0]
    )
    labels = jnp.where(ids_all[:, None] == text_ids[None, :], 1.0, -1.0).astype(jnp.float32)
    loss_all = -jnp.sum(jax.nn.log_sigmoid(labels * logits), axis=1)
    row_loss = lax.dynamic_slice_in_dim(loss_all, first_image, image_rows)
    coeffs = -logit_scale[0] * labels * jax.nn.sigmoid(-labels * logits)
    grad_image = jnp.dot(coeffs, text_all, precision=full_precision)
    own_coeffs = lax.dynamic_slice_in_dim(coeffs, position * text_rows, text_rows, 1)
    grad_text = jnp.dot(own_coeffs.T, image_unit, precision=full_precision)
    grad_texts = text_inverse * (
        grad_text - text_unit * jnp.sum(text_unit * grad_text, axis=1, keepdims=True)
    )
    grad_embed = (
        image_inverse
        * (grad_image - image_unit * jnp.sum(image_unit * grad_image, axis=1, keepdims=True))
    ).astype(jnp.bfloat16)
    grad_pooled = lax.dot_general(
        grad_embed, projection, (((1,), (1,)), ((), ())), preferred_element_type=jnp.float32
    ).astype(jnp.bfloat16)
    spread = jnp.dot(grad_pooled, w_down, preferred_element_type=jnp.float32) / cell_count
    own_spread = lax.dynamic_slice_in_dim(spread, first_image, image_rows)
    grad_pre = (
        (slope.reshape(image_rows, GRID * ROWS, hidden_share) * own_spread[:, None, :])
        .reshape(padded_rows, hidden_share)
        .astype(jnp.bfloat16)
    )
    grad_normed = lax.dot_general(
        grad_pre, w_up, (((1,), (1,)), ((), ())), preferred_element_type=jnp.float32
    ).reshape(padded.shape)
    part = conv_grads(padded, unit, inverse, gain_row, grad_normed)
    total = total_sum(part).transpose(1, 0, 2).reshape(TAP_ROWS, channels)
    grad_kernel = total[:cell_count].reshape(GRID, GRID, channels)
    grad_bias = total[cell_count]
    grad_gain = total[cell_count + 1]

    up_share = channels // loop_count
    grad_pooled_share = lax.dynamic_slice_in_dim(grad_pooled, position * up_share, up_share, 1)
    grad_down = lax.dot_general(
        grad_pooled_share, hidden_all, (((0,), (0,)), ((), ())), preferred_element_type=jnp.float32
    )
    proj_share = up_share // lax.axis_size("dp")
    proj_at = (lax.axis_index("dp") * loop_count + position) * proj_share
    pooled_share = lax.dynamic_slice_in_dim(pooled, proj_at, proj_share, 1)
    grad_proj = lax.dot_general(
        pooled_share, grad_embed, (((0,), (0,)), ((), ())), preferred_element_type=jnp.float32
    )
    grad_pre_all = (
        (slope_all.reshape(image_count, GRID * ROWS, hidden_share) * spread[:, None, :])
        .reshape(loop_count * padded_rows, hidden_share)
        .astype(jnp.bfloat16)
    )
    gain_share = lax.dynamic_slice_in_dim(norm_gain, position * up_share, up_share)
    normed_share = (unit_share * gain_share).astype(jnp.bfloat16)
    grad_up = lax.dot_general(
        normed_share,
        grad_pre_all,
        (((0,), (0,)), ((), ())),
        preferred_element_type=jnp.float32,
    )
    return (row_loss, grad_texts, grad_kernel, grad_bias, grad_gain, grad_up, grad_down, grad_proj)


def solution(mesh):
    placed = (
        P("loop", None, None, None),
        P("loop"),
        P("loop", None),
        P(),
        P(),
        P(),
        P(),
        P(None, "dp"),
        P(None, "dp"),
        P(),
        P(),
        P(),
    )
    return jax.shard_map(
        on_device,
        mesh=mesh,
        in_specs=placed,
        out_specs=(
            P("loop"),
            P("loop", None),
            P(),
            P(),
            P(),
            P("loop", "dp"),
            P("loop", "dp"),
            P(("dp", "loop"), None),
        ),
        check_vma=False,
    )
```
